32 devices in a mesh: row: 8 (over y, x, core), col: 4 (over z).
Axes of the slice: x: 2, y: 2, z: 4, core: 2. Of those that a mesh axis runs over, the one named last changes fastest.
Arguments:
- inputs: bfloat16 [1024, 6144], P('row', 'col'), may hold values from -6 to 6
- up_cells: int32 [4, 576], P('col'), may hold values from 0 to 2303, as said below
- up_blocks: bfloat16 [4, 576, 128, 128], P('col', 'row'), may hold values from -0.15625 to 0.15625
- down_cells: int32 [4, 576], P('col'), may hold values from 0 to 2303, as said below
- down_blocks: bfloat16 [4, 576, 128, 128], P('col', 'row'), may hold values from -0.078125 to 0.078125
- cotangent: bfloat16 [1024, 6144], P('row', 'col'), may hold values from -6 to 6
Outputs:
- output: bfloat16 [1024, 6144], P('row', 'col')
- input_grad: bfloat16 [1024, 6144], P('row', 'col')
- up_grad: bfloat16 [4, 576, 128, 128], P('col', 'row')
- down_grad: bfloat16 [4, 576, 128, 128], P('col', 'row')
The draws below stay inside these ranges and needn't reach their ends.
Inputs may be any that keep to these rules, and one draw needn't show every extreme that they name: Each row of up_cells names 576 distinct block numbers of its panel. Each row of down_cells names 576 distinct block numbers of its panel.
All inputs are finite; a program needn't handle non-finite values.
Results may differ from the reference program's by a relative error of at most 0.012.
Values may be sent and summed in bfloat16 or wider, within the bound.
No kernel may reach another device: no remote copies, remote signals or barrier semaphores. Data moves between devices by JAX's collectives and lax.ppermute only.
A program may use at most 192 MiB of HBM per device.

```python
import math
import jax
import jax.numpy as jnp
from jax import lax

D = 6144
H = 24576
BLK = 128
T_ROW = 128
TOKENS = 1024
NB_PANEL = 576
N_ROW = 8
N_COL = 4


def pick_cells(key):
    total_cells = D // BLK * (H // (BLK * N_COL))
    panel_keys = jax.random.split(key, N_COL)
    orders = jax.vmap(lambda panel_key: jax.random.permutation(panel_key, total_cells))(panel_keys)
    return orders[:, :NB_PANEL].astype(jnp.int32)


def draw_up_cells(key, part):
    return pick_cells(jax.random.fold_in(key, 11))


def draw_down_cells(key, part):
    return pick_cells(jax.random.fold_in(key, 23))


def shard_levels(own_key, shape, shards, least, largest):
    factor_of, own = 1.0, jax.random.fold_in(own_key, 6)
    for dim, blocks in shards:
        heights = jnp.exp(jax.random.uniform(jax.random.fold_in(own, dim), (blocks,), jnp.float32, least / len(shards), largest / len(shards)))
        factor_of = factor_of * jnp.repeat(heights, shape[dim] // blocks).reshape([-1 if axis == dim else 1 for axis in range(len(shape))])
    return factor_of


def noise(key, shape, width, reach, pieces=(), kind=jnp.bfloat16):
    drawn = jax.random.normal(key, shape, jnp.float32) * width
    if len(pieces) > 0:
        drawn = shard_levels(key, shape, pieces, -0.22, 0.18) * drawn
    return jnp.clip(drawn, min=-reach, max=reach).astype(kind)


def setup_inputs(seed: int = 0) -> dict:
    keys = jax.random.split(jax.random.key(seed), 7)
    return {
        "inputs": noise(keys[0], (TOKENS, D), 1.0, 6.0, ((0, 8), (1, 4))),
        "up_cells": draw_up_cells(jax.random.fold_in(keys[6], 71), 0),
        "up_blocks": noise(keys[2], (N_COL, NB_PANEL, BLK, BLK), (D // 4) ** -0.5, 0.15625, ((0, 4), (1, 8))),
        "down_cells": draw_down_cells(jax.random.fold_in(keys[6], 71), 0),
        "down_blocks": noise(keys[4], (N_COL, NB_PANEL, BLK, BLK), (H // 4) ** -0.5, 0.078125, ((0, 4), (1, 8))),
        "cotangent": noise(keys[5], (TOKENS, D), 1.0, 6.0, ((0, 8), (1, 4))),
    }


def spread(values, targets, how_many):
    onehot = (targets[:, None] == jnp.arange(how_many, dtype=jnp.int32)[None, :]).astype(values.dtype)
    return jnp.einsum('tnj,nc->tcj', values, onehot, precision=lax.Precision.HIGHEST)

def group_sum(lhs_rows, rhs_rows, factor):
    lhs_groups = lhs_rows.reshape(N_ROW, T_ROW, lhs_rows.shape[1], lhs_rows.shape[2])
    rhs_groups = rhs_rows.reshape(N_ROW, T_ROW, rhs_rows.shape[1], rhs_rows.shape[2])
    terms = jnp.einsum('rtnk,rtnj->rnkj', lhs_groups, rhs_groups) * factor
    rounded = lax.optimization_barrier(terms.astype(jnp.bfloat16))
    return lax.optimization_barrier(jnp.sum(rounded.astype(jnp.float32), axis=0)).astype(jnp.bfloat16)

def reference(inputs, up_cells, up_blocks, down_cells, down_blocks, cotangent):
    in_blocks = D // BLK
    hid_blocks = H // (BLK * N_COL)
    factor = 1.0 / math.sqrt(TOKENS)
    in_tiles = inputs.reshape(TOKENS, in_blocks, BLK)
    cot_tiles = cotangent.reshape(TOKENS, in_blocks, BLK)

    def panel_step(sums_so_far, element):
        cells_up, tiles_up, cells_down, tiles_down = element
        up_source = (cells_up // hid_blocks).astype(jnp.int32)
        up_target = (cells_up % hid_blocks).astype(jnp.int32)
        down_source = (cells_down // in_blocks).astype(jnp.int32)
        down_target = (cells_down % in_blocks).astype(jnp.int32)
        weights_up = tiles_up.astype(jnp.float32)
        weights_down = tiles_down.astype(jnp.float32)
        taken = jnp.take(in_tiles, up_source, axis=1).astype(jnp.float32)
        preact = spread(jnp.einsum('tnk,nkj->tnj', taken, weights_up), up_target, hid_blocks)
        sigmoid_val = jax.nn.sigmoid(preact)
        hidden = (preact * sigmoid_val).astype(jnp.bfloat16)
        derivative = sigmoid_val * (1.0 + preact * (1.0 - sigmoid_val))
        hid_taken = jnp.take(hidden, down_source, axis=1).astype(jnp.float32)
        partial_out = spread(jnp.einsum('tnk,nkj->tnj', hid_taken, weights_down), down_target, in_blocks)
        cot_taken = jnp.take(cot_tiles, down_target, axis=1).astype(jnp.float32)
        hidden_grad = spread(jnp.einsum('tnj,nkj->tnk', cot_taken, weights_down), down_source, hid_blocks)
        act_grad = (hidden_grad * derivative).astype(jnp.bfloat16)
        act_taken = jnp.take(act_grad, up_target, axis=1).astype(jnp.float32)
        partial_in = spread(jnp.einsum('tnj,nkj->tnk', act_taken, weights_up), up_source, in_blocks)
        down_part = group_sum(hid_taken, cot_taken, factor)
        up_part = group_sum(taken, act_taken, factor)
        out_round = lax.optimization_barrier(partial_out.astype(jnp.bfloat16))
        in_round = lax.optimization_barrier(partial_in.astype(jnp.bfloat16))
        new_sums = (sums_so_far[0] + out_round.astype(jnp.float32), sums_so_far[1] + in_round.astype(jnp.float32))
        return (new_sums, (up_part, down_part))
    zeros_init = jnp.zeros((TOKENS, in_blocks, BLK), jnp.float32)
    sums_final, grads = lax.scan(panel_step, (zeros_init, zeros_init), (up_cells, up_blocks, down_cells, down_blocks))
    output = sums_final[0].reshape(TOKENS, D).astype(jnp.bfloat16)
    input_grad = sums_final[1].reshape(TOKENS, D).astype(jnp.bfloat16)
    return (output, input_grad, grads[0], grads[1])
```

```python
import functools
import math

import jax
import jax.numpy as jnp
from jax import lax
from jax.experimental import pallas as pl
from jax.experimental.pallas import tpu as pltpu
from jax.sharding import PartitionSpec as P

D = 6144
H = 24576
ANY = pl.BlockSpec(memory_space=pl.ANY)
VMEM = pl.BlockSpec(memory_space=pltpu.VMEM)
DOT = functools.partial(lax.dot_general, preferred_element_type=jnp.float32)


def split(count, least):
    for parts in (3, 2):
        if count % parts == 0 and count // parts >= least:
            return count // parts
    return count


def spmm(src, dst, owners, pieces, weights, groups, n_src, n_dst, flip):
    nb, side = weights[0].shape[0], weights[0].shape[-1]
    nw = len(weights)
    rows = max(r + p.shape[0] for p, r, _ in pieces)
    per = rows // groups
    width = n_dst * side
    chunk = split(nb, 8)
    unroll = next(u for u in (8, 6, 4, 3, 2, 1) if chunk % u == 0)
    places = [(r, c, p.shape) for p, r, c in pieces]
    np_ = len(places)
    dims = (((1,), (1 if flip else 0,)), ((), ()))

    def body(src_ref, dst_ref, own_ref, *refs):
        p_refs, w_refs = refs[:np_], refs[np_ : np_ + nw]
        outs = refs[np_ + nw : np_ + nw + groups]
        xs, ws, acc, sem_x, sem_w = refs[np_ + nw + groups :]
        loads = [
            pltpu.make_async_copy(
                ref, xs.at[pl.ds(r, shape[0]), pl.ds(c, shape[1])], sem_x.at[n]
            )
            for n, (ref, (r, c, shape)) in enumerate(zip(p_refs, places))
        ]
        for load in loads:
            load.start()
        steps = []
        for w in range(nw):
            for t in range(0, nb, chunk):
                copy = pltpu.make_async_copy(
                    w_refs[w].at[pl.ds(t, chunk)], ws.at[pl.ds(w * nb + t, chunk)], sem_w.at[len(steps)]
                )
                copy.start()
                steps.append((w, t, copy))
        outs[0][...] = jnp.zeros_like(outs[0])
        acc[...] = jnp.zeros_like(acc)
        for load in loads:
            load.wait()
        for w, t, copy in steps:
            copy.wait()
            first = own_ref[w] * nb + t

            def run(g, carry, w=w, t=t, first=first):
                for u in range(unroll):
                    n = g * unroll + u
                    i = src_ref[first + n]
                    j = dst_ref[first + n]
                    x = xs[:, pl.ds(pl.multiple_of(i * side, side), side)]
                    part = DOT(x, ws[w * nb + t + n], dims)
                    at = pl.ds(pl.multiple_of(j * side, side), side)
                    outs[0][:, at] += part[:per]
                    if groups > 1:
                        acc[:, at] += part[per:]
                return carry

            lax.fori_loop(0, chunk // unroll, run, 0)
        for g in range(1, groups):
            outs[g][...] = acc[pl.ds((g - 1) * per, per), :].astype(jnp.bfloat16)

    flops = 2 * rows * side * side * nb * nw
    return pl.pallas_call(
        body,
        grid_spec=pltpu.PrefetchScalarGridSpec(
            num_scalar_prefetch=3,
            grid=(),
            in_specs=[ANY] * (np_ + nw),
            out_specs=[VMEM] * groups,
            scratch_shapes=[
                pltpu.VMEM((rows, n_src * side), jnp.bfloat16),
                pltpu.VMEM((nw * nb, side, side), jnp.bfloat16),
                pltpu.VMEM((max(groups - 1, 1) * per, width), jnp.float32),
                pltpu.SemaphoreType.DMA((np_,)),
                pltpu.SemaphoreType.DMA((nw * (nb // chunk),)),
            ],
        ),
        out_shape=[jax.ShapeDtypeStruct((per, width), jnp.float32)]
        + [jax.ShapeDtypeStruct((per, width), jnp.bfloat16)] * (groups - 1),
        cost_estimate=pl.CostEstimate(
            flops=8 * flops, bytes_accessed=2 * nw * nb * side * side, transcendentals=0
        ),
    )(src, dst, owners, *[p for p, _, _ in pieces], *weights)


def outer(lidx, ridx, owners, left, right, adds, nb, side, n_left, n_right, factor):
    nw = owners.shape[0]
    rows = max(r + p.shape[0] for p, r, _ in left)
    chunk = split(nb, 8)
    unroll = next(u for u in (8, 6, 4, 3, 2, 1) if chunk % u == 0)
    l_places = [(r, c, p.shape) for p, r, c in left]
    r_places = [(r, c, p.shape) for p, r, c in right]
    nl, nr, na = len(left), len(right), len(adds)
    per_w = nb // chunk

    def body(l_ref, r_ref, own_ref, *refs):
        lp, rp, ap = refs[:nl], refs[nl : nl + nr], refs[nl + nr : nl + nr + na]
        outs = refs[nl + nr + na : nl + nr + na + nw]
        ls, lt, rs, os, sem_l, sem_r, sem_o, *more = refs[nl + nr + na + nw :]
        loads = []
        for buf, sem, p_refs, places in ((ls, sem_l, lp, l_places), (rs, sem_r, rp, r_places)):
            for n, (ref, (r, c, shape)) in enumerate(zip(p_refs, places)):
                loads.append(
                    pltpu.make_async_copy(ref, buf.at[pl.ds(r, shape[0]), pl.ds(c, shape[1])], sem.at[n])
                )
                loads[-1].start()
        gets = []
        if na:
            ad, sem_a = more
            for w in range(nw):
                gets.append(pltpu.make_async_copy(ap[w], ad.at[pl.ds(w * nb, nb)], sem_a.at[w]))
                gets[-1].start()
        for load in loads[:nl]:
            load.wait()

        def turn(c, carry):
            at = pl.multiple_of(c * side, side)
            lt[pl.ds(at, side), :] = ls[:, pl.ds(at, side)].T
            return carry

        lax.fori_loop(0, n_left, turn, 0)
        for load in loads[nl:]:
            load.wait()
        puts = []
        for w in range(nw):
            if na:
                gets[w].wait()
            for t in range(0, nb, chunk):
                first = own_ref[w] * nb + t

                def run(g, carry, w=w, t=t, first=first):
                    for u in range(unroll):
                        n = g * unroll + u
                        i = l_ref[first + n]
                        j = r_ref[first + n]
                        a = lt[pl.ds(pl.multiple_of(i * side, side), side), :]
                        b = rs[:, pl.ds(pl.multiple_of(j * side, side), side)]
                        got = DOT(a, b, (((1,), (0,)), ((), ()))) * factor
                        at = w * nb + t + n
                        if na:
                            got = got + ad[at].astype(jnp.float32)
                        os[at] = got.astype(jnp.bfloat16)
                    return carry

                lax.fori_loop(0, chunk // unroll, run, 0)
                put = pltpu.make_async_copy(
                    os.at[pl.ds(w * nb + t, chunk)], outs[w].at[pl.ds(t, chunk)], sem_o.at[len(puts)]
                )
                put.start()
                puts.append(put)
        for put in puts:
            put.wait()

    scratch = [
        pltpu.VMEM((rows, n_left * side), jnp.bfloat16),
        pltpu.VMEM((n_left * side, rows), jnp.bfloat16),
        pltpu.VMEM((rows, n_right * side), jnp.bfloat16),
        pltpu.VMEM((nw * nb, side, side), jnp.bfloat16),
        pltpu.SemaphoreType.DMA((nl,)),
        pltpu.SemaphoreType.DMA((nr,)),
        pltpu.SemaphoreType.DMA((nw * per_w,)),
    ]
    if na:
        scratch += [pltpu.VMEM((nw * nb, side, side), jnp.bfloat16), pltpu.SemaphoreType.DMA((nw,))]
    return pl.pallas_call(
        body,
        grid_spec=pltpu.PrefetchScalarGridSpec(
            num_scalar_prefetch=3,
            grid=(),
            in_specs=[ANY] * (nl + nr + na),
            out_specs=[ANY] * nw,
            scratch_shapes=scratch,
        ),
        out_shape=[jax.ShapeDtypeStruct((nb, side, side), jnp.bfloat16)] * nw,
        cost_estimate=pl.CostEstimate(
            flops=16 * rows * side * side * nb * nw, bytes_accessed=4 * nw * nb * side * side, transcendentals=0
        ),
    )(lidx, ridx, owners, *[p for p, _, _ in left], *[p for p, _, _ in right], *adds)


def solution(mesh):
    n_row, n_col = mesh.shape["row"], mesh.shape["col"]
    sizes = {"a": 2, "b": n_row // 4, "k": 2}

    def coords(r):
        return {"a": r // (2 * sizes["b"]), "b": (r // 2) % sizes["b"], "k": r % 2}

    def index(a, b, k):
        return (a * sizes["b"] + b) * 2 + k

    def shift(x, axis, s):
        pairs = []
        for r in range(n_row):
            at = coords(r)
            at[axis] = (at[axis] + s) % sizes[axis]
            pairs.append((r, index(**at)))
        return lax.ppermute(x, "row", pairs)

    def gather(x, axis):
        return [x] + [shift(x, axis, s) for s in range(1, sizes[axis])]

    def col_shift(x, s):
        return lax.ppermute(x, "col", [(z, (z + s) % n_col) for z in range(n_col)])

    def shards(inputs, up_cells, up_blocks, down_cells, down_blocks, cotangent):
        nb, side = up_blocks.shape[1], up_blocks.shape[-1]
        rows = inputs.shape[0]
        part = inputs.shape[1]
        in_blocks = D // side
        hid_blocks = H // (side * n_col)
        share = in_blocks // n_col
        factor = 1.0 / math.sqrt(rows * n_row)
        up, down = up_blocks[0], down_blocks[0]
        row, z = lax.axis_index("row"), lax.axis_index("col")
        here = {"a": row // (2 * sizes["b"]), "b": (row // 2) % sizes["b"], "k": row % 2}

        def owner(axis, off, dk):
            at = dict(here)
            at[axis] = (at[axis] + sizes[axis] - off) % sizes[axis]
            at["k"] = (at["k"] + dk) % 2
            return index(**at)

        def near(block):
            return (z - block // share + n_col) % n_col * share + block % share

        def far(block):
            return (block // share - z + n_col) % n_col * share + block % share

        up_in, up_hid = up_cells[0] // hid_blocks, up_cells[0] % hid_blocks
        down_hid, down_in = down_cells[0] // in_blocks, down_cells[0] % in_blocks
        up_from, up_to = near(up_in), far(up_in)
        down_from, down_to = near(down_in), far(down_in)
        up_own = [owner("a", s, dk) for dk in range(2) for s in range(sizes["a"])]
        down_own = [owner("b", s, dk) for dk in range(2) for s in range(sizes["b"])]
        up_owners, down_owners = jnp.stack(up_own), jnp.stack(down_own)

        up_near = gather(up, "a")
        down_near = gather(down, "b")
        up_all = up_near + [shift(w, "k", 1) for w in up_near]
        down_all = down_near + [shift(w, "k", 1) for w in down_near]

        def spread(x, axis):
            both = jnp.concatenate(gather(x, axis), axis=0)
            return [(p, 0, s * part) for s, p in enumerate([both] + [col_shift(both, s) for s in range(1, n_col)])]

        in_pieces = spread(inputs, "b")
        cot_pieces = spread(cotangent, "a")

        pre_own, *pre_send = spmm(
            up_from, up_hid, up_owners, in_pieces, up_all, sizes["b"], in_blocks, hid_blocks, False
        )
        hg_own, *hg_send = spmm(
            down_from, down_hid, down_owners, cot_pieces, down_all, sizes["a"], in_blocks, hid_blocks, True
        )

        def collect(own, others, axis):
            total = own
            for g, other in enumerate(others, 1):
                total = total + shift(other, axis, -g).astype(jnp.float32)
            return total

        preact = collect(pre_own, pre_send, "b")
        sig = jax.nn.sigmoid(preact)
        hidden = (preact * sig).astype(jnp.bfloat16)
        derivative = sig * (1.0 + preact * (1.0 - sig))
        act = (collect(hg_own, hg_send, "a") * derivative).astype(jnp.bfloat16)

        hid_pieces = [(p, s * rows, 0) for s, p in enumerate(gather(hidden, "a"))]
        act_pieces = [(p, s * rows, 0) for s, p in enumerate(gather(act, "b"))]

        out_own, *out_send = spmm(
            down_hid, down_to, down_owners, hid_pieces, down_all, sizes["a"], hid_blocks, in_blocks, False
        )
        in_own, *in_send = spmm(
            up_hid, up_to, up_owners, act_pieces, up_all, sizes["b"], hid_blocks, in_blocks, True
        )

        def scatter(own, others, axis):
            total = collect(own, others, axis)
            final = total[:, :part]
            for s in range(1, n_col):
                piece = total[:, s * part : (s + 1) * part].astype(jnp.bfloat16)
                final = final + col_shift(piece, s).astype(jnp.float32)
            return final.astype(jnp.bfloat16)

        output = scatter(out_own, out_send, "a")
        input_grad = scatter(in_own, in_send, "b")

        def weight_grad(lidx, ridx, owners, left, right, n_left, n_right, axis):
            n = sizes[axis]
            run = functools.partial(
                outer, lidx, ridx, nb=nb, side=side, n_left=n_left, n_right=n_right, factor=factor
            )
            theirs = run(owners=owners[n:], left=left, right=right, adds=[])
            got = [shift(t, "k", 1) for t in theirs]
            mine = run(owners=owners[:n], left=left, right=right, adds=got)
            total = mine[0].astype(jnp.float32)
            for s in range(1, n):
                total = total + shift(mine[s], axis, -s).astype(jnp.float32)
            return total.astype(jnp.bfloat16)[None]

        down_grad = weight_grad(
            down_hid, down_from, down_owners, hid_pieces, cot_pieces, hid_blocks, in_blocks, "b"
        )
        up_grad = weight_grad(
            up_from, up_hid, up_owners, in_pieces, act_pieces, in_blocks, hid_blocks, "a"
        )
        return output, input_grad, up_grad, down_grad

    in_specs = (
        P("row", "col"),
        P("col", None),
        P("col", "row", None, None),
        P("col", None),
        P("col", "row", None, None),
        P("row", "col"),
    )
    out_specs = (
        P("row", "col"),
        P("row", "col"),
        P("col", "row", None, None),
        P("col", "row", None, None),
    )
    return jax.shard_map(shards, mesh=mesh, in_specs=in_specs, out_specs=out_specs, check_vma=False)
```
